256 devices in a mesh: seq: 64 (over z, x, core), head: 4 (over y).
Axes of the slice: x: 4, y: 4, z: 8, core: 2. Of those that a mesh axis runs over, the one named last changes fastest.
Arguments:
- queries: bfloat16 [65536, 4096], P('seq', 'head'), may hold values from -11 to 11
- keys: bfloat16 [65536, 1024], P('seq', 'head'), may hold values from -5 to 5
- values: bfloat16 [65536, 1024], P('seq', 'head'), may hold values from -6 to 6
- output_gradient: bfloat16 [65536, 4096], P('seq', 'head'), may hold values from -6 to 6
- rand_blocks: int32 [512, 3], P(('seq', 'head')), may hold values from 0 to 511, as said below
- global_ids: int32 [2], replicated, may hold values from 0 to 511, as said below
Outputs:
- grad_queries: bfloat16 [65536, 4096], P('seq', 'head')
- key_gradient: bfloat16 [65536, 1024], P('seq', 'head')
- value_gradient: bfloat16 [65536, 1024], P('seq', 'head')
The draws below stay inside these ranges and needn't reach their ends.
Inputs may be any that keep to these rules, and one draw needn't show every extreme that they name: `rand_blocks`: within each aligned run of 8 query blocks, the 24 random entries name at most 1 block of any one run of 8 key blocks, and exactly 1 of one such run. `global_ids`: Distinct; one of them is the last block, 511.
All inputs are finite; a program needn't handle non-finite values.
Results may differ from the reference program's by a relative error of at most 0.006.
Values may be sent and summed in bfloat16 or wider, within the bound.
No kernel may reach another device: no remote copies, remote signals or barrier semaphores. Data moves between devices by JAX's collectives and lax.ppermute only.
A program may use at most 256 MiB of HBM per device.

```python
import math
import jax
import jax.numpy as jnp
from jax import lax

BLOCK_TOKENS = 128
HEAD_SIZE = 128
QUERY_HEADS = 32
KEY_VALUE_HEADS = 8
NGLOB = 2
NRAND = 3
BLK_DEV = 8
SEQUENCE_BLOCKS = 512
SEQUENCE_TOKENS = 65536
KEY_BLOCK_COUNT = 8


def draw_keys(key, part):
    base_offset = jnp.clip(jax.random.normal(jax.random.fold_in(key, 1), (SEQUENCE_TOKENS, KEY_VALUE_HEADS, HEAD_SIZE), jnp.float32), -5.0, 5.0)
    return base_offset.reshape(SEQUENCE_TOKENS, KEY_VALUE_HEADS * HEAD_SIZE).astype(jnp.bfloat16)


def draw_queries(key, part):
    query_group_width = QUERY_HEADS // KEY_VALUE_HEADS
    base_offset = jnp.clip(jax.random.normal(jax.random.fold_in(key, 2), (SEQUENCE_TOKENS, KEY_VALUE_HEADS, query_group_width, HEAD_SIZE), jnp.float32), -5.0, 5.0)
    return base_offset.reshape(SEQUENCE_TOKENS, QUERY_HEADS * HEAD_SIZE).astype(jnp.bfloat16)


def draw_rand_blocks(key, part):
    owners_all = SEQUENCE_BLOCKS // BLK_DEV
    request_count = BLK_DEV * NRAND
    device_keys = jax.random.split(jax.random.fold_in(key, 11), owners_all)

    def one_device(dev_key):
        order_key, local_key = jax.random.split(dev_key)
        order = jax.random.permutation(order_key, owners_all)
        owner = order[jnp.arange(request_count) % owners_all]
        local = jax.random.randint(local_key, (request_count,), 0, BLK_DEV)
        return (owner * BLK_DEV + local).astype(jnp.int32)
    return jax.vmap(one_device)(device_keys).reshape(SEQUENCE_BLOCKS, NRAND).astype(jnp.int32)


def draw_global_ids(key, part):
    others = jax.random.permutation(jax.random.fold_in(key, 13), SEQUENCE_BLOCKS - 1)[:NGLOB - 1].astype(jnp.int32)
    listed = jnp.concatenate([jnp.full((1,), SEQUENCE_BLOCKS - 1, jnp.int32), others])
    order = jax.random.permutation(jax.random.fold_in(key, 14), NGLOB)
    return listed[order].astype(jnp.int32)


def block_scale(rng, shape, cuts, smallest, high):
    factor_of, own = 1.0, jax.random.fold_in(rng, 6)
    for position, shards_of in cuts:
        steps = jnp.exp(jax.random.uniform(jax.random.fold_in(own, position), (shards_of,), jnp.float32, smallest / len(cuts), high / len(cuts)))
        factor_of = factor_of * jnp.repeat(steps, shape[position] // shards_of).reshape([-1 if axis == position else 1 for axis in range(len(shape))])
    return factor_of


def normal_values(key, dims, width, most, pieces=(), held_as=jnp.bfloat16):
    values = jax.random.normal(key, dims, jnp.float32) * width
    if len(pieces) > 0:
        values = block_scale(key, dims, pieces, -0.22, 0.18) * values
    return jnp.clip(values, min=-most, max=most).astype(held_as)


def setup_inputs(seed: int = 0) -> dict:
    key_list = jax.random.split(jax.random.key(seed), 7)
    queries = draw_queries(jax.random.fold_in(key_list[6], 71), 0)
    keys = draw_keys(jax.random.fold_in(key_list[6], 71), 0)
    values = normal_values(key_list[2], (SEQUENCE_TOKENS, KEY_VALUE_HEADS * HEAD_SIZE), 1.0, 6.0, ((0, 64), (1, 4)))
    output_gradient = normal_values(key_list[3], (SEQUENCE_TOKENS, QUERY_HEADS * HEAD_SIZE), 1.0, 6.0, ((0, 64), (1, 4)))
    rand_blocks = draw_rand_blocks(jax.random.fold_in(key_list[6], 71), 0)
    global_ids = draw_global_ids(jax.random.fold_in(key_list[6], 71), 0)
    return {"queries": queries, "keys": keys, "values": values, "output_gradient": output_gradient, "rand_blocks": rand_blocks, "global_ids": global_ids}


def reference(queries, keys, values, output_gradient, rand_blocks, global_ids):
    score_scale = 1.0 / math.sqrt(HEAD_SIZE)
    query_group_width = QUERY_HEADS // KEY_VALUE_HEADS
    blocked_keys = keys.reshape(SEQUENCE_BLOCKS, BLOCK_TOKENS, KEY_VALUE_HEADS, HEAD_SIZE)
    blocked_values = values.reshape(SEQUENCE_BLOCKS, BLOCK_TOKENS, KEY_VALUE_HEADS, HEAD_SIZE)
    blocked_queries = queries.reshape(SEQUENCE_BLOCKS, BLOCK_TOKENS, KEY_VALUE_HEADS, query_group_width, HEAD_SIZE)
    output_grad_blocks = output_gradient.reshape(SEQUENCE_BLOCKS, BLOCK_TOKENS, KEY_VALUE_HEADS, query_group_width, HEAD_SIZE)
    whole_pos = jnp.arange(SEQUENCE_BLOCKS, dtype=jnp.int32)
    key_lists = jnp.concatenate([(whole_pos - 1)[:, None], whole_pos[:, None], (whole_pos + 1)[:, None], jnp.broadcast_to(global_ids[None, :], (SEQUENCE_BLOCKS, NGLOB)), rand_blocks], axis=1).astype(jnp.int32)
    list_valid = (key_lists >= 0) & (key_lists < SEQUENCE_BLOCKS)
    safe_lists = jnp.clip(key_lists, 0, SEQUENCE_BLOCKS - 1).astype(jnp.int32)

    def attend(carry, inputs):
        summed_key_grads, summed_value_grads = carry
        q_rows, g_rows, block_index_row, valid_row = inputs
        nearby_keys = blocked_keys[block_index_row].reshape(KEY_BLOCK_COUNT * BLOCK_TOKENS, KEY_VALUE_HEADS, HEAD_SIZE).astype(jnp.float32)
        nearby_values = blocked_values[block_index_row].reshape(KEY_BLOCK_COUNT * BLOCK_TOKENS, KEY_VALUE_HEADS, HEAD_SIZE).astype(jnp.float32)
        q_wide = q_rows.astype(jnp.float32)
        g_wide = g_rows.astype(jnp.float32)
        key_mask = jnp.repeat(valid_row, BLOCK_TOKENS)
        scores = jnp.einsum('qghd,kgd->ghqk', q_wide, nearby_keys) * score_scale
        masked = jnp.where(key_mask, scores, jnp.float32(-1e+30))
        top_score = lax.optimization_barrier(jnp.max(masked, axis=-1, keepdims=True))
        expo = jnp.where(key_mask, jnp.exp(masked - top_score), jnp.float32(0.0))
        probs = expo / lax.optimization_barrier(jnp.sum(expo, axis=-1, keepdims=True))
        dprobs = jnp.einsum('qghd,kgd->ghqk', g_wide, nearby_values)
        delta = lax.optimization_barrier(jnp.sum(probs * dprobs, axis=-1, keepdims=True))
        dscores = (probs * (dprobs - delta)).astype(jnp.bfloat16).astype(jnp.float32)
        probs_low = probs.astype(jnp.bfloat16).astype(jnp.float32)
        partial_values = jnp.einsum('ghqk,qghd->kgd', probs_low, g_wide)
        partial_keys = jnp.einsum('ghqk,qghd->kgd', dscores, q_wide) * score_scale
        dq_rows = (jnp.einsum('ghqk,kgd->qghd', dscores, nearby_keys) * score_scale).astype(jnp.bfloat16)
        attention_weight = valid_row[:, None, None, None]
        summed_key_grads = summed_key_grads.at[block_index_row].add(jnp.where(attention_weight, partial_keys.reshape(KEY_BLOCK_COUNT, BLOCK_TOKENS, KEY_VALUE_HEADS, HEAD_SIZE), jnp.float32(0.0)))
        summed_value_grads = summed_value_grads.at[block_index_row].add(jnp.where(attention_weight, partial_values.reshape(KEY_BLOCK_COUNT, BLOCK_TOKENS, KEY_VALUE_HEADS, HEAD_SIZE), jnp.float32(0.0)))
        return ((summed_key_grads, summed_value_grads), dq_rows)
    initial_zero_gradients = jnp.zeros((SEQUENCE_BLOCKS, BLOCK_TOKENS, KEY_VALUE_HEADS, HEAD_SIZE), jnp.float32)
    (summed_key_grads, summed_value_grads), dq_all = lax.scan(attend, (initial_zero_gradients, initial_zero_gradients), (blocked_queries, output_grad_blocks, safe_lists, list_valid))
    grad_queries = dq_all.reshape(SEQUENCE_TOKENS, QUERY_HEADS * HEAD_SIZE)
    key_gradient = summed_key_grads.reshape(SEQUENCE_TOKENS, KEY_VALUE_HEADS * HEAD_SIZE).astype(jnp.bfloat16)
    value_gradient = summed_value_grads.reshape(SEQUENCE_TOKENS, KEY_VALUE_HEADS * HEAD_SIZE).astype(jnp.bfloat16)
    return (grad_queries, key_gradient, value_gradient)
```

```python
import functools
import math

import jax
import jax.numpy as jnp
from jax import lax
from jax.experimental import pallas as pl
from jax.experimental.pallas import tpu as pltpu
from jax.sharding import Mesh, PartitionSpec as P

BLOCK = 128
DIM = 128
WIDE = 8
PIECE = BLOCK // WIDE
BLOCKS = 8
EXTRA = 4
NRAND = 3
SLOTS = EXTRA + BLOCKS * NRAND
POOL = BLOCKS + SLOTS
GROUP = 4
LANES = GROUP * BLOCK
LIST = 8
SCALE = 1.0 / math.sqrt(DIM)
LOG2E = math.log2(math.e)
VMEM_LIMIT = 56 * 1024 * 1024


def pick_kernel(index_ref, *refs, places):
    count = len(places)
    parts, out_ref, pool, sems = refs[:count], refs[count], refs[count + 1], refs[count + 2]
    copies = [
        pltpu.make_async_copy(part, pool.at[pl.ds(start, part.shape[0])], sems.at[n])
        for n, (part, start) in enumerate(zip(parts, places))
    ]
    for copy in copies:
        copy.start()
    for copy in copies:
        copy.wait()

    def body(i, carry):
        out_ref[i] = pool[index_ref[i]]
        return carry

    lax.fori_loop(0, out_ref.shape[0], body, 0, unroll=8)


def pick(index, parts, places, total):
    shape = (index.shape[0],) + parts[0].shape[1:]
    size = total * math.prod(parts[0].shape[1:]) * 2
    return pl.pallas_call(
        functools.partial(pick_kernel, places=places),
        out_shape=jax.ShapeDtypeStruct(shape, jnp.bfloat16),
        grid_spec=pltpu.PrefetchScalarGridSpec(
            num_scalar_prefetch=1,
            grid=(1,),
            in_specs=[pl.BlockSpec(memory_space=pl.ANY)] * len(parts),
            out_specs=pl.BlockSpec(shape, lambda i, index: (0, 0, 0)),
            scratch_shapes=[
                pltpu.VMEM((total,) + parts[0].shape[1:], jnp.bfloat16),
                pltpu.SemaphoreType.DMA((len(parts),)),
            ],
        ),
        compiler_params=pltpu.CompilerParams(vmem_limit_bytes=VMEM_LIMIT),
        cost_estimate=pl.CostEstimate(flops=0, bytes_accessed=2 * size, transcendentals=0),
        name="pick",
    )(index, *parts)


def spread_kernel(index_ref, x_ref, total_ref, low_ref, high_ref):
    rows = total_ref.shape[0]

    def clear(i, carry):
        total_ref[i] = jnp.zeros(total_ref.shape[1:], jnp.float32)
        return carry

    lax.fori_loop(0, rows, clear, 0, unroll=8)

    def body(i, carry):
        place = index_ref[i]
        total_ref[place] = total_ref[place] + x_ref[i].astype(jnp.float32)
        return carry

    lax.fori_loop(0, x_ref.shape[0], body, 0, unroll=4)
    half = low_ref.shape[0]

    def far(i, carry):
        low_ref[i] = total_ref[rows // 2 + i].astype(jnp.bfloat16)
        high_ref[i] = total_ref[rows // 2 + half + i].astype(jnp.bfloat16)
        return carry

    lax.fori_loop(0, half, far, 0, unroll=4)


def spread(index, x, total):
    tail = x.shape[1:]
    half = total // 16
    size = total * math.prod(tail) * 4

    def whole(shape):
        return pl.BlockSpec(shape, lambda i, index: (0, 0, 0))

    return pl.pallas_call(
        spread_kernel,
        out_shape=(
            jax.ShapeDtypeStruct((total,) + tail, jnp.float32),
            jax.ShapeDtypeStruct((half,) + tail, jnp.bfloat16),
            jax.ShapeDtypeStruct((half,) + tail, jnp.bfloat16),
        ),
        grid_spec=pltpu.PrefetchScalarGridSpec(
            num_scalar_prefetch=1,
            grid=(1,),
            in_specs=[whole(x.shape)],
            out_specs=(whole((total,) + tail), whole((half,) + tail), whole((half,) + tail)),
        ),
        compiler_params=pltpu.CompilerParams(vmem_limit_bytes=VMEM_LIMIT),
        cost_estimate=pl.CostEstimate(flops=0, bytes_accessed=2 * size, transcendentals=0),
        name="spread",
    )(index, x)


def attend_kernel(ends_ref, q_ref, g_ref, k_ref, v_ref, fetched_ref, *refs, alias):
    refs = refs[alias:]
    dq_ref, back_ref, dk_ref, dv_ref = refs[:4]
    kp, vp, kt, ak, av, sc, dp, ds, kl = refs[4:]
    b = pl.program_id(0)

    @pl.when(b == 0)
    def _():
        for i in range(BLOCKS):
            kp[i] = k_ref[i * BLOCK : (i + 1) * BLOCK, :]
            vp[i] = v_ref[i * BLOCK : (i + 1) * BLOCK, :]

        def fill(s, carry):
            kp[BLOCKS + s] = fetched_ref[:, s, :, :DIM].reshape(BLOCK, DIM)
            vp[BLOCKS + s] = fetched_ref[:, s, :, DIM:].reshape(BLOCK, DIM)
            return carry

        lax.fori_loop(0, SLOTS, fill, 0)

        def turn(s, carry):
            kt[s] = kp[s].T
            ak[s] = jnp.zeros((BLOCK, DIM), jnp.float32)
            av[s] = jnp.zeros((BLOCK, DIM), jnp.float32)
            return carry

        lax.fori_loop(0, POOL, turn, 0)

    pool = [
        jnp.where(b == 0, BLOCKS, b - 1),
        b,
        jnp.where(b == BLOCKS - 1, BLOCKS + 1, b + 1),
        BLOCKS + 2,
        BLOCKS + 3,
    ] + [BLOCKS + EXTRA + NRAND * b + j for j in range(NRAND)]
    q = jnp.concatenate([q_ref[:, h * DIM : (h + 1) * DIM] for h in range(GROUP)], axis=0)
    g = jnp.concatenate([g_ref[:, h * DIM : (h + 1) * DIM] for h in range(GROUP)], axis=0)
    rows = (((1,), (1,)), ((), ()))
    top = None
    for c in range(LIST):
        s = lax.dot_general(kp[pool[c]], q, rows, preferred_element_type=jnp.float32)
        if c == 0:
            s = jnp.where(jnp.logical_and(b == 0, ends_ref[0] > 0), jnp.float32(-1e30), s)
        if c == 2:
            s = jnp.where(
                jnp.logical_and(b == BLOCKS - 1, ends_ref[1] > 0), jnp.float32(-1e30), s
            )
        sc[c * BLOCK : (c + 1) * BLOCK, :] = s
        here = jnp.max(s, axis=0, keepdims=True)
        top = here if top is None else jnp.maximum(top, here)
        dp[c * BLOCK : (c + 1) * BLOCK, :] = lax.dot_general(
            vp[pool[c]], g, rows, preferred_element_type=jnp.float32
        )
        kl[:, c * BLOCK : (c + 1) * BLOCK] = kt[pool[c]]
    top = top * (SCALE * LOG2E)
    norm = jnp.zeros((1, LANES), jnp.float32)
    dot = jnp.zeros((1, LANES), jnp.float32)
    for c in range(LIST):
        at = slice(c * BLOCK, (c + 1) * BLOCK)
        e = jnp.exp2(sc[at, :] * (SCALE * LOG2E) - top)
        sc[at, :] = e
        norm = norm + jnp.sum(e, axis=0, keepdims=True)
        dot = dot + jnp.sum(e * dp[at, :], axis=0, keepdims=True)
    inverse = 1.0 / norm
    delta = dot * inverse
    for c in range(LIST):
        at = slice(c * BLOCK, (c + 1) * BLOCK)
        probs = sc[at, :] * inverse
        grad = (probs * (dp[at, :] - delta)).astype(jnp.bfloat16)
        ds[at, :] = grad
        av[pool[c]] += jnp.dot(probs.astype(jnp.bfloat16), g, preferred_element_type=jnp.float32)
        ak[pool[c]] += jnp.dot(grad, q, preferred_element_type=jnp.float32)
    dqt = jnp.dot(kl[...], ds[...], preferred_element_type=jnp.float32) * SCALE
    for h in range(GROUP):
        dq_ref[:, h * DIM : (h + 1) * DIM] = dqt[:, h * BLOCK : (h + 1) * BLOCK].T.astype(
            jnp.bfloat16
        )

    @pl.when(b == BLOCKS - 1)
    def _():
        for i in range(BLOCKS):
            dk_ref[i * BLOCK : (i + 1) * BLOCK, :] = ak[i] * SCALE
            dv_ref[i * BLOCK : (i + 1) * BLOCK, :] = av[i]

        def emit(s, carry):
            one = (ak[BLOCKS + s] * SCALE).astype(jnp.bfloat16)
            two = av[BLOCKS + s].astype(jnp.bfloat16)
            back_ref[:, s, :, :DIM] = one.reshape(WIDE, PIECE, DIM)
            back_ref[:, s, :, DIM:] = two.reshape(WIDE, PIECE, DIM)
            return carry

        lax.fori_loop(0, SLOTS, emit, 0)


def attend(ends, queries, output_gradient, keys, values, fetched, head, dq=None):
    alias = dq is not None
    cols = GROUP * DIM
    row = pl.BlockSpec((BLOCK, cols), lambda b, ends: (b, head))
    own = pl.BlockSpec((BLOCKS * BLOCK, DIM), lambda b, ends: (0, head))
    moved = pl.BlockSpec(fetched.shape, lambda b, ends: (0, 0, 0, 0))
    local = pl.BlockSpec((BLOCKS * BLOCK, DIM), lambda b, ends: (0, 0))
    grad = jax.ShapeDtypeStruct((BLOCKS * BLOCK, DIM), jnp.float32)
    args = [ends, queries, output_gradient, keys, values, fetched] + ([dq] if alias else [])
    return pl.pallas_call(
        functools.partial(attend_kernel, alias=int(alias)),
        out_shape=(
            jax.ShapeDtypeStruct(queries.shape, jnp.bfloat16),
            jax.ShapeDtypeStruct(fetched.shape, jnp.bfloat16),
            grad,
            grad,
        ),
        grid_spec=pltpu.PrefetchScalarGridSpec(
            num_scalar_prefetch=1,
            grid=(BLOCKS,),
            in_specs=[row, row, own, own, moved] + [pl.BlockSpec(memory_space=pl.ANY)] * alias,
            out_specs=(row, moved, local, local),
            scratch_shapes=[
                pltpu.VMEM((POOL, BLOCK, DIM), jnp.bfloat16),
                pltpu.VMEM((POOL, BLOCK, DIM), jnp.bfloat16),
                pltpu.VMEM((POOL, DIM, BLOCK), jnp.bfloat16),
                pltpu.VMEM((POOL, BLOCK, DIM), jnp.float32),
                pltpu.VMEM((POOL, BLOCK, DIM), jnp.float32),
                pltpu.VMEM((LIST * BLOCK, LANES), jnp.float32),
                pltpu.VMEM((LIST * BLOCK, LANES), jnp.float32),
                pltpu.VMEM((LIST * BLOCK, LANES), jnp.bfloat16),
                pltpu.VMEM((DIM, LIST * BLOCK), jnp.bfloat16),
            ],
        ),
        input_output_aliases={6: 0} if alias else {},
        compiler_params=pltpu.CompilerParams(vmem_limit_bytes=VMEM_LIMIT),
        cost_estimate=pl.CostEstimate(
            flops=BLOCKS * LIST * BLOCK * LANES * DIM * 10 * 2,
            bytes_accessed=8 * 1024 * 1024,
            transcendentals=BLOCKS * LIST * BLOCK * LANES,
        ),
        name="attend",
    )(*args)


def ring_gather(x, ring):
    up = [(i, (i + 1) % ring) for i in range(ring)]
    down = [(i, (i - 1) % ring) for i in range(ring)]
    rows = x.shape[0]
    parts, places = [x], [0]
    a = b = x
    for step in range(1, ring // 2):
        a = lax.ppermute(a, "z", up)
        b = lax.ppermute(b, "z", down)
        parts += [a, b]
        places += [(ring - step) * rows, step * rows]
    half = rows // 2
    a = lax.ppermute(a[:half], "z", up)
    b = lax.ppermute(b[half:], "z", down)
    parts += [a, b]
    places += [ring // 2 * rows, ring // 2 * rows + half]
    return parts, tuple(places)


def ring_reduce(total, low, high, ring):
    up = [(i, (i + 1) % ring) for i in range(ring)]
    down = [(i, (i - 1) % ring) for i in range(ring)]
    half = low.shape[0]
    rows = 2 * half
    far = ring // 2

    def place(n):
        return total[n * rows : (n + 1) * rows]

    a = lax.ppermute(low, "z", up).astype(jnp.float32)
    b = lax.ppermute(high, "z", down).astype(jnp.float32)
    here, there = place(far - 1), place(far + 1)
    a = jnp.concatenate([here[:half] + a, here[half:]], axis=0).astype(jnp.bfloat16)
    b = jnp.concatenate([there[:half], there[half:] + b], axis=0).astype(jnp.bfloat16)
    for step in range(2, far):
        a = lax.ppermute(a, "z", up).astype(jnp.float32)
        b = lax.ppermute(b, "z", down).astype(jnp.float32)
        a = (place(far - step) + a).astype(jnp.bfloat16)
        b = (place(far + step) + b).astype(jnp.bfloat16)
    a = lax.ppermute(a, "z", up).astype(jnp.float32)
    b = lax.ppermute(b, "z", down).astype(jnp.float32)
    return (place(0) + a + b).astype(jnp.bfloat16)


def exchange(x):
    return lax.all_to_all(x, "w", split_axis=0, concat_axis=0, tiled=True)


def local(queries, keys, values, output_gradient, rand_blocks, global_ids):
    ring = lax.axis_size("z")
    my_z, my_w = lax.axis_index("z"), lax.axis_index("w")
    heads = keys.shape[1] // DIM
    plane = WIDE * BLOCKS
    last = ring * plane - 1
    wide = 2 * DIM

    pieces = []
    for head in range(heads):
        at = slice(head * DIM, (head + 1) * DIM)
        both = jnp.concatenate([keys[:, at], values[:, at]], axis=1)
        pieces.append(
            both.reshape(BLOCKS, WIDE, PIECE, wide)
            .transpose(1, 0, 2, 3)
            .reshape(plane, PIECE, wide)
        )

    lists = lax.all_gather(rand_blocks, ("w", "head"), axis=0, tiled=True)
    lists = lists.reshape(WIDE, BLOCKS * NRAND)
    first = (my_z * WIDE + jnp.arange(WIDE, dtype=jnp.int32)) * BLOCKS
    wanted = jnp.concatenate(
        [
            jnp.maximum(first - 1, 0)[:, None],
            jnp.minimum(first + BLOCKS, last)[:, None],
            jnp.broadcast_to(global_ids[None, :], (WIDE, 2)),
            lists,
        ],
        axis=1,
    ).reshape(WIDE * SLOTS)
    where = (wanted // plane - my_z + ring) % ring * plane + wanted % plane
    me = my_z * WIDE + my_w
    ends = jnp.stack([me == 0, me == ring * WIDE - 1]).astype(jnp.int32)

    dq = None
    sums = []
    for head in range(heads):
        spreadout = exchange(pieces[head])
        parts, places = ring_gather(spreadout, ring)
        chosen = pick(where, parts, places, ring * plane)
        fetched = exchange(chosen)
        dq, back, dk, dv = attend(
            ends,
            queries,
            output_gradient,
            keys,
            values,
            fetched.reshape(WIDE, SLOTS, PIECE, wide),
            head,
            dq,
        )
        returned = exchange(back.reshape(WIDE * SLOTS, PIECE, wide))
        total, low, high = spread(where, returned, ring * plane)
        mine = exchange(ring_reduce(total, low, high, ring))
        mine = (
            mine.reshape(WIDE, BLOCKS, PIECE, wide)
            .transpose(1, 0, 2, 3)
            .reshape(BLOCKS * BLOCK, wide)
            .astype(jnp.float32)
        )
        sums.append((dk + mine[:, :DIM], dv + mine[:, DIM:]))
    key_gradient = jnp.concatenate([one for one, _ in sums], axis=1).astype(jnp.bfloat16)
    value_gradient = jnp.concatenate([two for _, two in sums], axis=1).astype(jnp.bfloat16)
    return dq, key_gradient, value_gradient


def solution(mesh):
    seq, head = mesh.devices.shape
    split = Mesh(mesh.devices.reshape(seq // WIDE, WIDE, head), ("z", "w", "head"))
    rows = P(("z", "w"), "head")
    return jax.shard_map(
        local,
        mesh=split,
        in_specs=(rows, rows, rows, rows, P(("z", "w", "head"), None), P()),
        out_specs=(rows, rows, rows),
        check_vma=False,
    )
```

```python
import functools
import math

import jax
import jax.numpy as jnp
from jax import lax
from jax.experimental import pallas as pl
from jax.experimental.pallas import tpu as pltpu
from jax.sharding import Mesh, PartitionSpec as P

BLOCK = 128
DIM = 128
WIDE = 8
PIECE = BLOCK // WIDE
BLOCKS = 8
EXTRA = 4
NRAND = 3
SLOTS = EXTRA + BLOCKS * NRAND
POOL = BLOCKS + SLOTS
GROUP = 4
LANES = GROUP * BLOCK
LIST = 8
SCALE = 1.0 / math.sqrt(DIM)
LOG2E = math.log2(math.e)
PAIR = 4
VMEM_LIMIT = 56 * 1024 * 1024


def pick_kernel(index_ref, *refs, places):
    count = len(places)
    parts, out_ref, pool, sems = refs[:count], refs[count], refs[count + 1], refs[count + 2]
    copies = [
        pltpu.make_async_copy(part, pool.at[pl.ds(start, part.shape[0])], sems.at[n])
        for n, (part, start) in enumerate(zip(parts, places))
    ]
    for copy in copies:
        copy.start()
    for copy in copies:
        copy.wait()

    def body(i, carry):
        out_ref[i] = pool[index_ref[i]]
        return carry

    lax.fori_loop(0, out_ref.shape[0], body, 0, unroll=8)


def pick(index, parts, places, total):
    shape = (index.shape[0],) + parts[0].shape[1:]
    size = total * math.prod(parts[0].shape[1:]) * 2
    return pl.pallas_call(
        functools.partial(pick_kernel, places=places),
        out_shape=jax.ShapeDtypeStruct(shape, jnp.bfloat16),
        grid_spec=pltpu.PrefetchScalarGridSpec(
            num_scalar_prefetch=1,
            grid=(1,),
            in_specs=[pl.BlockSpec(memory_space=pl.ANY)] * len(parts),
            out_specs=pl.BlockSpec(shape, lambda i, index: (0, 0, 0)),
            scratch_shapes=[
                pltpu.VMEM((total,) + parts[0].shape[1:], jnp.bfloat16),
                pltpu.SemaphoreType.DMA((len(parts),)),
            ],
        ),
        compiler_params=pltpu.CompilerParams(vmem_limit_bytes=VMEM_LIMIT),
        cost_estimate=pl.CostEstimate(flops=0, bytes_accessed=2 * size, transcendentals=0),
        name="pick",
    )(index, *parts)


def spread_kernel(index_ref, x_ref, total_ref):
    def clear(i, carry):
        total_ref[i] = jnp.zeros(total_ref.shape[1:], jnp.float32)
        return carry

    def body(i, carry):
        place = index_ref[i]
        total_ref[place] = total_ref[place] + x_ref[i].astype(jnp.float32)
        return carry

    lax.fori_loop(0, total_ref.shape[0], clear, 0, unroll=8 if total_ref.shape[0] % 8 == 0 else 5)
    lax.fori_loop(0, x_ref.shape[0], body, 0, unroll=8)


def spread_far_kernel(index_ref, x_ref, low_ref, high_ref, total_ref):
    spread_kernel(index_ref, x_ref, total_ref)
    half = low_ref.shape[0]
    low_ref[...] = total_ref[:half].astype(jnp.bfloat16)
    high_ref[...] = total_ref[half : 2 * half].astype(jnp.bfloat16)


def whole(shape):
    return pl.BlockSpec(shape, lambda i, index: (0,) * len(shape))


def spread(index, x, total):
    shape = (total,) + x.shape[1:]
    return pl.pallas_call(
        spread_kernel,
        out_shape=jax.ShapeDtypeStruct(shape, jnp.float32),
        grid_spec=pltpu.PrefetchScalarGridSpec(
            num_scalar_prefetch=1,
            grid=(1,),
            in_specs=[whole(x.shape)],
            out_specs=whole(shape),
        ),
        compiler_params=pltpu.CompilerParams(vmem_limit_bytes=VMEM_LIMIT),
        cost_estimate=pl.CostEstimate(flops=0, bytes_accessed=20 << 20, transcendentals=0),
        name="spread",
    )(index, x)


def spread_far(index, x, rows):
    shape = (rows // 2,) + x.shape[1:]
    return pl.pallas_call(
        spread_far_kernel,
        out_shape=[jax.ShapeDtypeStruct(shape, jnp.bfloat16)] * 2,
        grid_spec=pltpu.PrefetchScalarGridSpec(
            num_scalar_prefetch=1,
            grid=(1,),
            in_specs=[whole(x.shape)],
            out_specs=[whole(shape)] * 2,
            scratch_shapes=[pltpu.VMEM((rows + 1,) + x.shape[1:], jnp.float32)],
        ),
        compiler_params=pltpu.CompilerParams(vmem_limit_bytes=VMEM_LIMIT),
        cost_estimate=pl.CostEstimate(flops=0, bytes_accessed=12 << 20, transcendentals=0),
        name="spread_far",
    )(index, x)


def attend_kernel(ends_ref, q_ref, g_ref, k_ref, v_ref, fetched_ref, *refs, alias):
    refs = refs[alias:]
    dq_ref, back_ref, dk_ref, dv_ref = refs[:4]
    kp, vp, kt, ak, av, sc, dp, ds, kl, tk, tv = refs[4:]
    b = pl.program_id(0)

    @pl.when(b == 0)
    def _():
        for i in range(BLOCKS):
            kp[i] = k_ref[i * BLOCK : (i + 1) * BLOCK, :]
            vp[i] = v_ref[i * BLOCK : (i + 1) * BLOCK, :]

        def fill(s, carry):
            kp[BLOCKS + s] = fetched_ref[:, s, :, :DIM].reshape(BLOCK, DIM)
            vp[BLOCKS + s] = fetched_ref[:, s, :, DIM:].reshape(BLOCK, DIM)
            return carry

        lax.fori_loop(0, SLOTS, fill, 0, unroll=4)

        def turn(s, carry):
            kt[s] = kp[s].T
            ak[s] = jnp.zeros((BLOCK, DIM), jnp.float32)
            av[s] = jnp.zeros((BLOCK, DIM), jnp.float32)
            return carry

        lax.fori_loop(0, POOL, turn, 0, unroll=4)

    rows = (((1,), (1,)), ((), ()))

    def block(n):
        at_b = PAIR * b + n
        pool = [
            jnp.where(at_b == 0, BLOCKS, at_b - 1),
            at_b,
            jnp.where(at_b == BLOCKS - 1, BLOCKS + 1, at_b + 1),
            BLOCKS + 2,
            BLOCKS + 3,
        ] + [BLOCKS + EXTRA + NRAND * at_b + j for j in range(NRAND)]
        span = slice(n * BLOCK, (n + 1) * BLOCK)
        q = jnp.concatenate([q_ref[span, h * DIM : (h + 1) * DIM] for h in range(GROUP)], axis=0)
        g = jnp.concatenate([g_ref[span, h * DIM : (h + 1) * DIM] for h in range(GROUP)], axis=0)
        held = {}

        def scores(c):
            s = lax.dot_general(kp[pool[c]], q, rows, preferred_element_type=jnp.float32)
            if c == 0:
                void = jnp.logical_and(at_b == 0, ends_ref[0] > 0)
                s = jnp.where(void, jnp.float32(-1e30), s)
            if c == 2:
                void = jnp.logical_and(at_b == BLOCKS - 1, ends_ref[1] > 0)
                s = jnp.where(void, jnp.float32(-1e30), s)
            sc[n, c] = s
            here = jnp.max(s, axis=0, keepdims=True)
            held["top"] = here if c == 0 else jnp.maximum(held["top"], here)
            kl[n, :, c * BLOCK : (c + 1) * BLOCK] = kt[pool[c]]

        def weights(c):
            if c == 0:
                held["top"] = held["top"] * (SCALE * LOG2E)
                held["norm"] = jnp.zeros((1, LANES), jnp.float32)
                held["dot"] = jnp.zeros((1, LANES), jnp.float32)
            d = lax.dot_general(vp[pool[c]], g, rows, preferred_element_type=jnp.float32)
            e = jnp.exp2(sc[n, c] * (SCALE * LOG2E) - held["top"])
            sc[n, c] = e
            dp[n, c] = d
            held["norm"] += jnp.sum(e, axis=0, keepdims=True)
            held["dot"] += jnp.sum(e * d, axis=0, keepdims=True)

        def grads(c):
            if c == 0:
                held["inverse"] = 1.0 / held["norm"]
                held["delta"] = held["dot"] * held["inverse"]
            probs = sc[n, c] * held["inverse"]
            grad = (probs * (dp[n, c] - held["delta"])).astype(jnp.bfloat16)
            ds[n, c * BLOCK : (c + 1) * BLOCK, :] = grad
            tv[n, c] = jnp.dot(probs.astype(jnp.bfloat16), g, preferred_element_type=jnp.float32)
            tk[n, c] = jnp.dot(grad, q, preferred_element_type=jnp.float32)

        def finish():
            dqt = jnp.dot(kl[n], ds[n], preferred_element_type=jnp.float32) * SCALE
            for h in range(GROUP):
                dq_ref[span, h * DIM : (h + 1) * DIM] = dqt[
                    :, h * BLOCK : (h + 1) * BLOCK
                ].T.astype(jnp.bfloat16)
            for c in range(LIST):
                av[pool[c]] += tv[n, c]
                ak[pool[c]] += tk[n, c]

        return scores, weights, grads, finish

    blocks = [block(n) for n in range(PAIR)]
    for step in range(PAIR + 2):
        for c in range(LIST):
            for phase in range(3):
                if 0 <= step - phase < PAIR:
                    blocks[step - phase][phase](c)
        if step >= 2:
            blocks[step - 2][3]()

    @pl.when(b == BLOCKS // PAIR - 1)
    def _():
        for i in range(BLOCKS):
            dk_ref[i * BLOCK : (i + 1) * BLOCK, :] = ak[i] * SCALE
            dv_ref[i * BLOCK : (i + 1) * BLOCK, :] = av[i]

        def emit(s, carry):
            one = (ak[BLOCKS + s] * SCALE).astype(jnp.bfloat16)
            two = av[BLOCKS + s].astype(jnp.bfloat16)
            back_ref[:, s, :, :DIM] = one.reshape(WIDE, PIECE, DIM)
            back_ref[:, s, :, DIM:] = two.reshape(WIDE, PIECE, DIM)
            return carry

        lax.fori_loop(0, SLOTS, emit, 0, unroll=4)


def attend(ends, queries, output_gradient, keys, values, fetched, head, dq=None):
    alias = dq is not None
    cols = GROUP * DIM
    row = pl.BlockSpec((PAIR * BLOCK, cols), lambda b, ends: (b, head))
    own = pl.BlockSpec((BLOCKS * BLOCK, DIM), lambda b, ends: (0, head))
    moved = pl.BlockSpec(fetched.shape, lambda b, ends: (0, 0, 0, 0))
    local = pl.BlockSpec((BLOCKS * BLOCK, DIM), lambda b, ends: (0, 0))
    grad = jax.ShapeDtypeStruct((BLOCKS * BLOCK, DIM), jnp.float32)
    args = [ends, queries, output_gradient, keys, values, fetched] + ([dq] if alias else [])
    return pl.pallas_call(
        functools.partial(attend_kernel, alias=int(alias)),
        out_shape=(
            jax.ShapeDtypeStruct(queries.shape, jnp.bfloat16),
            jax.ShapeDtypeStruct(fetched.shape, jnp.bfloat16),
            grad,
            grad,
        ),
        grid_spec=pltpu.PrefetchScalarGridSpec(
            num_scalar_prefetch=1,
            grid=(BLOCKS // PAIR,),
            in_specs=[row, row, own, own, moved] + [pl.BlockSpec(memory_space=pl.ANY)] * alias,
            out_specs=(row, moved, local, local),
            scratch_shapes=[
                pltpu.VMEM((POOL, BLOCK, DIM), jnp.bfloat16),
                pltpu.VMEM((POOL, BLOCK, DIM), jnp.bfloat16),
                pltpu.VMEM((POOL, DIM, BLOCK), jnp.bfloat16),
                pltpu.VMEM((POOL, BLOCK, DIM), jnp.float32),
                pltpu.VMEM((POOL, BLOCK, DIM), jnp.float32),
                pltpu.VMEM((PAIR, LIST, BLOCK, LANES), jnp.float32),
                pltpu.VMEM((PAIR, LIST, BLOCK, LANES), jnp.float32),
                pltpu.VMEM((PAIR, LIST * BLOCK, LANES), jnp.bfloat16),
                pltpu.VMEM((PAIR, DIM, LIST * BLOCK), jnp.bfloat16),
                pltpu.VMEM((PAIR, LIST, BLOCK, DIM), jnp.float32),
                pltpu.VMEM((PAIR, LIST, BLOCK, DIM), jnp.float32),
            ],
        ),
        input_output_aliases={6: 0} if alias else {},
        compiler_params=pltpu.CompilerParams(vmem_limit_bytes=VMEM_LIMIT),
        cost_estimate=pl.CostEstimate(
            flops=BLOCKS * LIST * BLOCK * LANES * DIM * 10 * 2,
            bytes_accessed=8 * 1024 * 1024,
            transcendentals=BLOCKS * LIST * BLOCK * LANES,
        ),
        name="attend",
    )(*args)


def after(x, *others):
    return lax.optimization_barrier((x, others))[0]


def ring_pairs(ring):
    up = [(i, (i + 1) % ring) for i in range(ring)]
    down = [(i, (i - 1) % ring) for i in range(ring)]
    return up, down


def ring_gather(x, ring, others):
    up, down = ring_pairs(ring)
    rows = x.shape[0]
    half = rows // 2
    parts, places, steps = [x], [0], []
    ups = [x[:half], x[half:]]
    downs = list(ups)
    for step in range(1, ring // 2 + 1):
        if step in others:
            ready = others[step](steps)
            ups = [after(one, ready) for one in ups]
            downs = [after(one, ready) for one in downs]
        if step == ring // 2:
            ups[0] = lax.ppermute(ups[0], "z", up)
            downs[1] = lax.ppermute(downs[1], "z", down)
            parts += [ups[0], downs[1]]
            places += [step * rows, step * rows + half]
            break
        for n in range(2):
            ups[n] = lax.ppermute(ups[n], "z", up)
            downs[n] = lax.ppermute(downs[n], "z", down)
            parts += [ups[n], downs[n]]
            places += [(ring - step) * rows + n * half, step * rows + n * half]
        steps.append((*ups, *downs))
    return parts, tuple(places), steps


def ring_reduce(total, low, high, ring):
    up, down = ring_pairs(ring)
    half = low.shape[0]
    rows = 2 * half
    far = ring // 2

    def place(n):
        return total[n * rows : (n + 1) * rows]

    def send(a, b):
        a, b = lax.ppermute(a, "z", up), lax.ppermute(b, "z", down)
        a, b = lax.optimization_barrier((a, b))
        return a.astype(jnp.float32), b.astype(jnp.float32)

    a, b = send(low, high)
    a = jnp.pad(a, ((0, half), (0, 0), (0, 0)))
    b = jnp.pad(b, ((half, 0), (0, 0), (0, 0)))
    for step in range(1, far):
        a = (place(far - step) + a).astype(jnp.bfloat16)
        b = (place(far + step) + b).astype(jnp.bfloat16)
        a, b = send(a, b)
    return (place(0) + a + b).astype(jnp.bfloat16)


def exchange(x):
    return lax.all_to_all(x, "w", split_axis=0, concat_axis=0, tiled=True)


def local(queries, keys, values, output_gradient, rand_blocks, global_ids):
    ring = lax.axis_size("z")
    my_z, my_w = lax.axis_index("z"), lax.axis_index("w")
    heads = keys.shape[1] // DIM
    plane = WIDE * BLOCKS
    last = ring * plane - 1
    wide = 2 * DIM

    pieces = []
    for head in range(heads):
        at = slice(head * DIM, (head + 1) * DIM)
        both = jnp.concatenate([keys[:, at], values[:, at]], axis=1)
        pieces.append(
            both.reshape(BLOCKS, WIDE, PIECE, wide)
            .transpose(1, 0, 2, 3)
            .reshape(plane, PIECE, wide)
        )

    spreadout = [exchange(pieces[0])]
    mine = rand_blocks.reshape(1, -1)
    peers = WIDE * lax.axis_size("head")
    lists = lax.all_to_all(
        jnp.broadcast_to(after(mine, spreadout[0]), (peers, mine.shape[1])),
        ("w", "head"),
        split_axis=0,
        concat_axis=0,
        tiled=True,
    ).reshape(WIDE, BLOCKS * NRAND)
    first = (my_z * WIDE + jnp.arange(WIDE, dtype=jnp.int32)) * BLOCKS
    wanted = jnp.concatenate(
        [
            jnp.maximum(first - 1, 0)[:, None],
            jnp.minimum(first + BLOCKS, last)[:, None],
            jnp.broadcast_to(global_ids[None, :], (WIDE, 2)),
            lists,
        ],
        axis=1,
    ).reshape(WIDE * SLOTS)
    where = (wanted // plane - my_z + ring) % ring * plane + wanted % plane
    far = jnp.where(where // plane == ring // 2, where % plane, plane)
    me = my_z * WIDE + my_w
    ends = jnp.stack([me == 0, me == ring * WIDE - 1]).astype(jnp.int32)

    def send_next(steps):
        spreadout.append(exchange(after(pieces[len(spreadout)], steps[0])))
        return spreadout[-1]

    dq = None
    found = []
    last_step = ()
    for head in range(heads):
        others = {2: lambda steps: lists} if head == 0 else {}
        if head + 1 < heads:
            others[3] = send_next
        parts, places, steps = ring_gather(after(spreadout[head], last_step), ring, others)
        last_step = steps[-1]
        found.append(exchange(pick(where, parts, places, ring * plane)))
    sums = []
    for head in range(heads):
        fetched = found[head].reshape(WIDE, SLOTS, PIECE, wide)
        dq, back, dk, dv = attend(
            ends, queries, output_gradient, keys, values, fetched, head, dq
        )
        returned = exchange(back.reshape(WIDE * SLOTS, PIECE, wide))
        low, high = spread_far(far, returned, plane)
        total = spread(where, after(returned, low), ring * plane)
        mine = exchange(ring_reduce(total, low, high, ring))
        mine = (
            mine.reshape(WIDE, BLOCKS, PIECE, wide)
            .transpose(1, 0, 2, 3)
            .reshape(BLOCKS * BLOCK, wide)
            .astype(jnp.float32)
        )
        sums.append((dk + mine[:, :DIM], dv + mine[:, DIM:]))
    key_gradient = jnp.concatenate([one for one, _ in sums], axis=1).astype(jnp.bfloat16)
    value_gradient = jnp.concatenate([two for _, two in sums], axis=1).astype(jnp.bfloat16)
    return dq, key_gradient, value_gradient


def solution(mesh):
    seq, head = mesh.devices.shape
    split = Mesh(mesh.devices.reshape(seq // WIDE, WIDE, head), ("z", "w", "head"))
    rows = P(("z", "w"), "head")
    return jax.shard_map(
        local,
        mesh=split,
        in_specs=(rows, rows, rows, rows, P(("z", "w", "head"), None), P()),
        out_specs=(rows, rows, rows),
        check_vma=False,
    )
```

```python
import functools
import math

import jax
import jax.numpy as jnp
from jax import lax
from jax.experimental import pallas as pl
from jax.experimental.pallas import tpu as pltpu
from jax.sharding import Mesh, PartitionSpec as P

BLOCK = 128
DIM = 128
WIDE = 8
PIECE = BLOCK // WIDE
BLOCKS = 8
EXTRA = 4
NRAND = 3
SLOTS = EXTRA + BLOCKS * NRAND
POOL = BLOCKS + SLOTS
GROUP = 4
LANES = GROUP * BLOCK
LIST = 8
SCALE = 1.0 / math.sqrt(DIM)
LOG2E = math.log2(math.e)
PAIR = 4
VMEM_LIMIT = 56 * 1024 * 1024


def pick_kernel(index_ref, *refs, places):
    count = len(places)
    parts, out_ref, pool, sems = refs[:count], refs[count], refs[count + 1], refs[count + 2]
    copies = [
        pltpu.make_async_copy(part, pool.at[pl.ds(start, part.shape[0])], sems.at[n])
        for n, (part, start) in enumerate(zip(parts, places))
    ]
    for copy in copies:
        copy.start()
    for copy in copies:
        copy.wait()

    def body(i, carry):
        out_ref[i] = pool[index_ref[i]]
        return carry

    lax.fori_loop(0, out_ref.shape[0], body, 0, unroll=8)


def pick(index, parts, places, total):
    shape = (index.shape[0],) + parts[0].shape[1:]
    size = total * math.prod(parts[0].shape[1:]) * 2
    return pl.pallas_call(
        functools.partial(pick_kernel, places=places),
        out_shape=jax.ShapeDtypeStruct(shape, jnp.bfloat16),
        grid_spec=pltpu.PrefetchScalarGridSpec(
            num_scalar_prefetch=1,
            grid=(1,),
            in_specs=[pl.BlockSpec(memory_space=pl.ANY)] * len(parts),
            out_specs=pl.BlockSpec(shape, lambda i, index: (0, 0, 0)),
            scratch_shapes=[
                pltpu.VMEM((total,) + parts[0].shape[1:], jnp.bfloat16),
                pltpu.SemaphoreType.DMA((len(parts),)),
            ],
        ),
        compiler_params=pltpu.CompilerParams(vmem_limit_bytes=VMEM_LIMIT),
        cost_estimate=pl.CostEstimate(flops=0, bytes_accessed=2 * size, transcendentals=0),
        name="pick",
    )(index, *parts)


def spread_kernel(index_ref, x_ref, total_ref):
    def clear(i, carry):
        total_ref[i] = jnp.zeros(total_ref.shape[1:], jnp.float32)
        return carry

    def body(i, carry):
        place = index_ref[i]
        total_ref[place] = total_ref[place] + x_ref[i].astype(jnp.float32)
        return carry

    lax.fori_loop(0, total_ref.shape[0], clear, 0, unroll=8 if total_ref.shape[0] % 8 == 0 else 5)
    lax.fori_loop(0, x_ref.shape[0], body, 0, unroll=8)


def spread_far_kernel(index_ref, x_ref, low_ref, high_ref, total_ref):
    spread_kernel(index_ref, x_ref, total_ref)
    half = low_ref.shape[0]
    low_ref[...] = total_ref[:half].astype(jnp.bfloat16)
    high_ref[...] = total_ref[half : 2 * half].astype(jnp.bfloat16)


def whole(shape):
    return pl.BlockSpec(shape, lambda i, index: (0,) * len(shape))


def spread(index, x, total):
    shape = (total,) + x.shape[1:]
    return pl.pallas_call(
        spread_kernel,
        out_shape=jax.ShapeDtypeStruct(shape, jnp.float32),
        grid_spec=pltpu.PrefetchScalarGridSpec(
            num_scalar_prefetch=1,
            grid=(1,),
            in_specs=[whole(x.shape)],
            out_specs=whole(shape),
        ),
        compiler_params=pltpu.CompilerParams(vmem_limit_bytes=VMEM_LIMIT),
        cost_estimate=pl.CostEstimate(flops=0, bytes_accessed=20 << 20, transcendentals=0),
        name="spread",
    )(index, x)


def spread_far(index, x, rows):
    shape = (rows // 2,) + x.shape[1:]
    return pl.pallas_call(
        spread_far_kernel,
        out_shape=[jax.ShapeDtypeStruct(shape, jnp.bfloat16)] * 2,
        grid_spec=pltpu.PrefetchScalarGridSpec(
            num_scalar_prefetch=1,
            grid=(1,),
            in_specs=[whole(x.shape)],
            out_specs=[whole(shape)] * 2,
            scratch_shapes=[pltpu.VMEM((rows + 1,) + x.shape[1:], jnp.float32)],
        ),
        compiler_params=pltpu.CompilerParams(vmem_limit_bytes=VMEM_LIMIT),
        cost_estimate=pl.CostEstimate(flops=0, bytes_accessed=12 << 20, transcendentals=0),
        name="spread_far",
    )(index, x)


def attend_kernel(ends_ref, q_ref, g_ref, k_ref, v_ref, fetched_ref, *refs, alias):
    refs = refs[alias:]
    dq_ref, back_ref, dk_ref, dv_ref = refs[:4]
    kp, vp, kt, ak, av, sc, dp, ds, kl, tk, tv = refs[4:]
    b = pl.program_id(0)

    @pl.when(b == 0)
    def _():
        for i in range(BLOCKS):
            kp[i] = k_ref[i * BLOCK : (i + 1) * BLOCK, :]
            vp[i] = v_ref[i * BLOCK : (i + 1) * BLOCK, :]

        def fill(s, carry):
            kp[BLOCKS + s] = fetched_ref[:, s, :, :DIM].reshape(BLOCK, DIM)
            vp[BLOCKS + s] = fetched_ref[:, s, :, DIM:].reshape(BLOCK, DIM)
            return carry

        lax.fori_loop(0, SLOTS, fill, 0, unroll=4)

        def turn(s, carry):
            kt[s] = kp[s].T
            ak[s] = jnp.zeros((BLOCK, DIM), jnp.float32)
            av[s] = jnp.zeros((BLOCK, DIM), jnp.float32)
            return carry

        lax.fori_loop(0, POOL, turn, 0, unroll=4)

    rows = (((1,), (1,)), ((), ()))

    def block(n):
        at_b = PAIR * b + n
        pool = [
            jnp.where(at_b == 0, BLOCKS, at_b - 1),
            at_b,
            jnp.where(at_b == BLOCKS - 1, BLOCKS + 1, at_b + 1),
            BLOCKS + 2,
            BLOCKS + 3,
        ] + [BLOCKS + EXTRA + NRAND * at_b + j for j in range(NRAND)]
        span = slice(n * BLOCK, (n + 1) * BLOCK)
        q = jnp.concatenate([q_ref[span, h * DIM : (h + 1) * DIM] for h in range(GROUP)], axis=0)
        g = jnp.concatenate([g_ref[span, h * DIM : (h + 1) * DIM] for h in range(GROUP)], axis=0)
        held = {}

        def scores(c):
            s = lax.dot_general(kp[pool[c]], q, rows, preferred_element_type=jnp.float32)
            if c == 0:
                void = jnp.logical_and(at_b == 0, ends_ref[0] > 0)
                s = jnp.where(void, jnp.float32(-1e30), s)
            if c == 2:
                void = jnp.logical_and(at_b == BLOCKS - 1, ends_ref[1] > 0)
                s = jnp.where(void, jnp.float32(-1e30), s)
            sc[n, c] = s
            here = jnp.max(s, axis=0, keepdims=True)
            held["top"] = here if c == 0 else jnp.maximum(held["top"], here)
            kl[n, :, c * BLOCK : (c + 1) * BLOCK] = kt[pool[c]]

        def weights(c):
            if c == 0:
                held["top"] = held["top"] * (SCALE * LOG2E)
                held["norm"] = jnp.zeros((1, LANES), jnp.float32)
                held["dot"] = jnp.zeros((1, LANES), jnp.float32)
            d = lax.dot_general(vp[pool[c]], g, rows, preferred_element_type=jnp.float32)
            e = jnp.exp2(sc[n, c] * (SCALE * LOG2E) - held["top"])
            sc[n, c] = e
            dp[n, c] = d
            held["norm"] += jnp.sum(e, axis=0, keepdims=True)
            held["dot"] += jnp.sum(e * d, axis=0, keepdims=True)

        def grads(c):
            if c == 0:
                held["inverse"] = 1.0 / held["norm"]
                held["delta"] = held["dot"] * held["inverse"]
            probs = sc[n, c] * held["inverse"]
            grad = (probs * (dp[n, c] - held["delta"])).astype(jnp.bfloat16)
            ds[n, c * BLOCK : (c + 1) * BLOCK, :] = grad
            tv[n, c] = jnp.dot(probs.astype(jnp.bfloat16), g, preferred_element_type=jnp.float32)
            tk[n, c] = jnp.dot(grad, q, preferred_element_type=jnp.float32)

        def finish():
            dqt = jnp.dot(kl[n], ds[n], preferred_element_type=jnp.float32) * SCALE
            for h in range(GROUP):
                dq_ref[span, h * DIM : (h + 1) * DIM] = dqt[
                    :, h * BLOCK : (h + 1) * BLOCK
                ].T.astype(jnp.bfloat16)
            for c in range(LIST):
                av[pool[c]] += tv[n, c]
                ak[pool[c]] += tk[n, c]

        return scores, weights, grads, finish

    blocks = [block(n) for n in range(PAIR)]
    for step in range(PAIR + 2):
        for c in range(LIST):
            for phase in range(3):
                if 0 <= step - phase < PAIR:
                    blocks[step - phase][phase](c)
        if step >= 2:
            blocks[step - 2][3]()

    @pl.when(b == BLOCKS // PAIR - 1)
    def _():
        for i in range(BLOCKS):
            dk_ref[i * BLOCK : (i + 1) * BLOCK, :] = ak[i] * SCALE
            dv_ref[i * BLOCK : (i + 1) * BLOCK, :] = av[i]

        def emit(s, carry):
            one = (ak[BLOCKS + s] * SCALE).astype(jnp.bfloat16)
            two = av[BLOCKS + s].astype(jnp.bfloat16)
            back_ref[:, s, :, :DIM] = one.reshape(WIDE, PIECE, DIM)
            back_ref[:, s, :, DIM:] = two.reshape(WIDE, PIECE, DIM)
            return carry

        lax.fori_loop(0, SLOTS, emit, 0, unroll=4)


def attend(ends, queries, output_gradient, keys, values, fetched, head, dq=None):
    alias = dq is not None
    cols = GROUP * DIM
    row = pl.BlockSpec((PAIR * BLOCK, cols), lambda b, ends: (b, head))
    own = pl.BlockSpec((BLOCKS * BLOCK, DIM), lambda b, ends: (0, head))
    moved = pl.BlockSpec(fetched.shape, lambda b, ends: (0, 0, 0, 0))
    local = pl.BlockSpec((BLOCKS * BLOCK, DIM), lambda b, ends: (0, 0))
    grad = jax.ShapeDtypeStruct((BLOCKS * BLOCK, DIM), jnp.float32)
    args = [ends, queries, output_gradient, keys, values, fetched] + ([dq] if alias else [])
    return pl.pallas_call(
        functools.partial(attend_kernel, alias=int(alias)),
        out_shape=(
            jax.ShapeDtypeStruct(queries.shape, jnp.bfloat16),
            jax.ShapeDtypeStruct(fetched.shape, jnp.bfloat16),
            grad,
            grad,
        ),
        grid_spec=pltpu.PrefetchScalarGridSpec(
            num_scalar_prefetch=1,
            grid=(BLOCKS // PAIR,),
            in_specs=[row, row, own, own, moved] + [pl.BlockSpec(memory_space=pl.ANY)] * alias,
            out_specs=(row, moved, local, local),
            scratch_shapes=[
                pltpu.VMEM((POOL, BLOCK, DIM), jnp.bfloat16),
                pltpu.VMEM((POOL, BLOCK, DIM), jnp.bfloat16),
                pltpu.VMEM((POOL, DIM, BLOCK), jnp.bfloat16),
                pltpu.VMEM((POOL, BLOCK, DIM), jnp.float32),
                pltpu.VMEM((POOL, BLOCK, DIM), jnp.float32),
                pltpu.VMEM((PAIR, LIST, BLOCK, LANES), jnp.float32),
                pltpu.VMEM((PAIR, LIST, BLOCK, LANES), jnp.float32),
                pltpu.VMEM((PAIR, LIST * BLOCK, LANES), jnp.bfloat16),
                pltpu.VMEM((PAIR, DIM, LIST * BLOCK), jnp.bfloat16),
                pltpu.VMEM((PAIR, LIST, BLOCK, DIM), jnp.float32),
                pltpu.VMEM((PAIR, LIST, BLOCK, DIM), jnp.float32),
            ],
        ),
        input_output_aliases={6: 0} if alias else {},
        compiler_params=pltpu.CompilerParams(vmem_limit_bytes=VMEM_LIMIT),
        cost_estimate=pl.CostEstimate(
            flops=BLOCKS * LIST * BLOCK * LANES * DIM * 10 * 2,
            bytes_accessed=8 * 1024 * 1024,
            transcendentals=BLOCKS * LIST * BLOCK * LANES,
        ),
        name="attend",
    )(*args)


def after(x, *others):
    return lax.optimization_barrier((x, others))[0]


def ring_pairs(ring):
    up = [(i, (i + 1) % ring) for i in range(ring)]
    down = [(i, (i - 1) % ring) for i in range(ring)]
    return up, down


def ring_gather(x, ring, others):
    up, down = ring_pairs(ring)
    rows = x.shape[0]
    half = rows // 2
    parts, places, steps = [x], [0], []
    ups = [x[:half], x[half:]]
    downs = list(ups)
    for step in range(1, ring // 2 + 1):
        if step in others:
            ready = others[step](steps)
            ups = [after(one, ready) for one in ups]
            downs = [after(one, ready) for one in downs]
        if step == ring // 2:
            ups[0] = lax.ppermute(ups[0], "z", up)
            downs[1] = lax.ppermute(downs[1], "z", down)
            parts += [ups[0], downs[1]]
            places += [step * rows, step * rows + half]
            break
        for n in range(2):
            ups[n] = lax.ppermute(ups[n], "z", up)
            downs[n] = lax.ppermute(downs[n], "z", down)
            parts += [ups[n], downs[n]]
            places += [(ring - step) * rows + n * half, step * rows + n * half]
        steps.append((*ups, *downs))
    return parts, tuple(places), steps


def ring_reduce(total, low, high, ring):
    up, down = ring_pairs(ring)
    half = low.shape[0]
    rows = 2 * half
    far = ring // 2

    def place(n):
        return total[n * rows : (n + 1) * rows]

    def send(a, b):
        a, b = lax.ppermute(a, "z", up), lax.ppermute(b, "z", down)
        a, b = lax.optimization_barrier((a, b))
        return a.astype(jnp.float32), b.astype(jnp.float32)

    a, b = send(low, high)
    a = jnp.pad(a, ((0, half), (0, 0), (0, 0)))
    b = jnp.pad(b, ((half, 0), (0, 0), (0, 0)))
    second = None
    for step in range(1, far):
        a = (place(far - step) + a).astype(jnp.bfloat16)
        b = (place(far + step) + b).astype(jnp.bfloat16)
        a, b = send(a, b)
        if step == 1:
            second = (a, b)
    return (place(0) + a + b).astype(jnp.bfloat16), second


def exchange(x):
    return lax.all_to_all(x, "w", split_axis=0, concat_axis=0, tiled=True)


def local(queries, keys, values, output_gradient, rand_blocks, global_ids):
    ring = lax.axis_size("z")
    my_z, my_w = lax.axis_index("z"), lax.axis_index("w")
    heads = keys.shape[1] // DIM
    plane = WIDE * BLOCKS
    last = ring * plane - 1
    wide = 2 * DIM

    pieces = []
    for head in range(heads):
        at = slice(head * DIM, (head + 1) * DIM)
        both = jnp.concatenate([keys[:, at], values[:, at]], axis=1)
        pieces.append(
            both.reshape(BLOCKS, WIDE, PIECE, wide)
            .transpose(1, 0, 2, 3)
            .reshape(plane, PIECE, wide)
        )

    spreadout = [exchange(pieces[0])]
    mine = rand_blocks.reshape(1, -1)
    peers = WIDE * lax.axis_size("head")
    lists = lax.all_to_all(
        jnp.broadcast_to(after(mine, spreadout[0]), (peers, mine.shape[1])),
        ("w", "head"),
        split_axis=0,
        concat_axis=0,
        tiled=True,
    ).reshape(WIDE, BLOCKS * NRAND)
    first = (my_z * WIDE + jnp.arange(WIDE, dtype=jnp.int32)) * BLOCKS
    wanted = jnp.concatenate(
        [
            jnp.maximum(first - 1, 0)[:, None],
            jnp.minimum(first + BLOCKS, last)[:, None],
            jnp.broadcast_to(global_ids[None, :], (WIDE, 2)),
            lists,
        ],
        axis=1,
    ).reshape(WIDE * SLOTS)
    where = (wanted // plane - my_z + ring) % ring * plane + wanted % plane
    far = jnp.where(where // plane == ring // 2, where % plane, plane)
    me = my_z * WIDE + my_w
    ends = jnp.stack([me == 0, me == ring * WIDE - 1]).astype(jnp.int32)

    def send_next(steps):
        spreadout.append(exchange(after(pieces[len(spreadout)], steps[0])))
        return spreadout[-1]

    dq = None
    found = []
    last_step = ()
    for head in range(heads):
        others = {2: lambda steps: lists} if head == 0 else {}
        if head + 1 < heads:
            others[3] = send_next
        parts, places, steps = ring_gather(after(spreadout[head], last_step), ring, others)
        last_step = steps[-1]
        found.append(exchange(pick(where, parts, places, ring * plane)))
    sums = []
    second = ()
    for head in range(heads):
        fetched = found[head].reshape(WIDE, SLOTS, PIECE, wide)
        dq, back, dk, dv = attend(
            ends, queries, output_gradient, keys, values, fetched, head, dq
        )
        returned = exchange(back.reshape(WIDE * SLOTS, PIECE, wide))
        low, high = spread_far(far, returned, plane)
        total = spread(where, after(returned, low), ring * plane)
        low, high = after(low, second), after(high, second)
        mine, second = ring_reduce(total, low, high, ring)
        mine = exchange(mine)
        mine = (
            mine.reshape(WIDE, BLOCKS, PIECE, wide)
            .transpose(1, 0, 2, 3)
            .reshape(BLOCKS * BLOCK, wide)
            .astype(jnp.float32)
        )
        sums.append((dk + mine[:, :DIM], dv + mine[:, DIM:]))
    key_gradient = jnp.concatenate([one for one, _ in sums], axis=1).astype(jnp.bfloat16)
    value_gradient = jnp.concatenate([two for _, two in sums], axis=1).astype(jnp.bfloat16)
    return dq, key_gradient, value_gradient


def solution(mesh):
    seq, head = mesh.devices.shape
    split = Mesh(mesh.devices.reshape(seq // WIDE, WIDE, head), ("z", "w", "head"))
    rows = P(("z", "w"), "head")
    return jax.shard_map(
        local,
        mesh=split,
        in_specs=(rows, rows, rows, rows, P(("z", "w", "head"), None), P()),
        out_specs=(rows, rows, rows),
        check_vma=False,
    )
```
